256 devices in a mesh: st: 64 (over x, z, y_lo), ta: 4 (over y_hi, core).
Axes of the slice: x: 4, y: 4 (y_hi: 2, y_lo: 2; y = y_hi * 2 + y_lo), z: 8, core: 2. Of those that a mesh axis runs over, the one named last changes fastest.
Arguments:
- samples: bfloat16 [1024, 128, 8192], P('st', 'ta'), may hold values from -6 to 6
- coefficients: float32 [16, 8192], replicated, may hold values from -1.5 to 1.5
Outputs:
- visibilities: bfloat16 [256, 2, 1024, 1024], P(('st', 'ta'))
The draws below stay inside these ranges and needn't reach their ends.
All inputs are finite; a program needn't handle non-finite values.
Results may differ from the reference program's by a relative error of at most 0.0056.
Values may be sent and summed in bfloat16 or wider, within the bound.
A program may use at most 128 MiB of HBM per device.

```python
import math
import jax
import jax.numpy as jnp
from jax import lax

NFFT = 8192
TAPS = 16
IN_DEV = 16
CH0 = 1024
INPUTS = 1024
FRAMES = 128
CH = 256


def shard_levels(own_key, extent, split, least, largest):
    loudness, own = 1.0, jax.random.fold_in(own_key, 6)
    for position, shards_of in split:
        heights = jnp.exp(jax.random.uniform(jax.random.fold_in(own, position), (shards_of,), jnp.float32, least / len(split), largest / len(split)))
        loudness = loudness * jnp.repeat(heights, extent[position] // shards_of).reshape([-1 if axis == position else 1 for axis in range(len(extent))])
    return loudness


def normal_values(stream_key, extent, deviation, bound, shards=(), kind=jnp.bfloat16):
    result = deviation * jax.random.normal(stream_key, extent, jnp.float32)
    if shards:
        result = result * shard_levels(stream_key, extent, shards, -0.22, 0.18)
    return jnp.clip(result, -bound, bound).astype(kind)


def setup_inputs(seed: int = 0) -> dict:
    keys = jax.random.split(jax.random.key(seed), 3)
    return {
        "samples": normal_values(keys[0], (INPUTS, FRAMES, NFFT), 1.0, 6.0, ((0, 64), (1, 4))),
        "coefficients": normal_values(keys[1], (TAPS, NFFT), 0.25, 1.5, (), jnp.float32),
    }


def phase_table(frame_len, channel_count, first_channel):
    positions = jnp.arange(frame_len, dtype=jnp.int32)[:, None]
    channels = (first_channel + jnp.arange(channel_count, dtype=jnp.int32))[None, :]
    phases = (positions * channels) % frame_len
    angles = (2.0 * math.pi / frame_len) * phases.astype(jnp.float32)
    scale = jnp.float32(frame_len ** -0.5)
    stacked = jnp.stack([jnp.cos(angles) * scale, -jnp.sin(angles) * scale], axis=2)
    return stacked.reshape(frame_len, 2 * channel_count)


def filter_frames(extended, coefficients, frame_count):
    total_sum = jnp.zeros((extended.shape[0], frame_count, extended.shape[2]), jnp.float32)
    for tap_index in range(coefficients.shape[0]):
        window = extended[:, tap_index:tap_index + frame_count, :].astype(jnp.float32)
        total_sum = total_sum + coefficients[tap_index][None, None, :] * window
    return total_sum


def channelize_rows(filtered, table):
    return jnp.einsum("ifk,kc->cif", filtered, table, precision=lax.Precision.HIGHEST)


def correlate(channel_spectra):
    real_part = channel_spectra[0]
    imag_part = channel_spectra[1]
    left_rows = jnp.concatenate([jnp.concatenate([real_part, imag_part], 1), jnp.concatenate([imag_part, -real_part], 1)], 0)
    right_rows = jnp.concatenate([real_part, imag_part], 1)
    product = lax.dot_general(left_rows, right_rows, (((1,), (1,)), ((), ())), preferred_element_type=jnp.float32)
    return (product / jnp.float32(real_part.shape[1])).reshape(2, real_part.shape[0], real_part.shape[0]).astype(jnp.bfloat16)


def reference(samples, coefficients):
    table = phase_table(NFFT, CH, CH0)
    block_count = INPUTS // IN_DEV

    def channelize(input_block):
        zero_frames = jnp.zeros((IN_DEV, TAPS - 1, NFFT), jnp.bfloat16)
        extended = jnp.concatenate([input_block, zero_frames], 1)
        return channelize_rows(filter_frames(extended, coefficients, FRAMES), table).astype(jnp.bfloat16)

    spectra = lax.map(channelize, samples.reshape(block_count, IN_DEV, FRAMES, NFFT))
    spectra = spectra.transpose(1, 0, 2, 3).reshape(CH, 2, INPUTS, FRAMES)
    return lax.map(correlate, spectra)
```

```python
import functools
import math

import jax
import jax.numpy as jnp
import numpy as np
from jax import lax
from jax.experimental import pallas as pl
from jax.experimental.pallas import tpu as pltpu
from jax.sharding import PartitionSpec as P

CH0 = 1024
MESH_IDS = pl.DeviceIdType.MESH
BF16 = jnp.bfloat16
F32 = jnp.float32

NFFT = 8192
TAPS = 16
INPUTS_HERE = 16
FRAMES_HERE = 32
CHANNELS = 256
BINS = 24
HALF = 8
QUARTER = NFFT // 4
CHUNK = 256
STEPS = QUARTER // CHUNK


def _as_bf16(values):
    return np.asarray(values, np.float32).astype(BF16)


def _high_low(values):
    high = _as_bf16(values)
    return high, _as_bf16(values - high.astype(np.float64))


def _bin_angles():
    return 2.0 * np.pi * (np.arange(BINS) + 0.5) / (2 * BINS)


def _forward_matrix():
    angles = _bin_angles()[:, None] * np.arange(FRAMES_HERE)[None, :]
    parts = np.stack([np.cos(angles), -np.sin(angles)])
    block = np.zeros((2, HALF, BINS, HALF, FRAMES_HERE))
    for i in range(HALF):
        block[:, i, :, i, :] = parts
    return block.reshape(2 * HALF * BINS, HALF * FRAMES_HERE)


def _tap_matrix():
    angles = _bin_angles()[:, None] * np.arange(TAPS)[None, :]
    taps = np.concatenate([np.cos(angles), np.sin(angles)])
    high, low = _high_low(taps)
    return np.concatenate([high, high, low], 1)


def _inverse_matrices():
    scale = (2.0 / (2 * BINS)) * NFFT ** -0.5
    frames = np.arange(FRAMES_HERE)
    angles = _bin_angles()[:, None] * frames[None, :]
    own = scale * np.stack([np.cos(angles), -np.sin(angles)])
    before = _bin_angles()[:, None] * (frames - FRAMES_HERE)[None, :]
    halo = scale * np.stack([np.cos(before), -np.sin(before)])
    halo[:, :, : FRAMES_HERE - (TAPS - 1)] = 0.0
    out = []
    for parity in range(2):
        placed = halo if parity == 0 else np.roll(halo, -FRAMES_HERE // 2, axis=2)
        rows = np.zeros((2, 2, 2, FRAMES_HERE, 2, 2, 2, BINS))
        for p in range(2):
            for ri in range(2):
                rows[0, p, ri, :, ri, p] = np.moveaxis(own, 2, 0)
                rows[1, p, ri, :, ri, p] = np.moveaxis(placed, 2, 0)
        high, low = _high_low(rows.reshape(8 * FRAMES_HERE, 8 * BINS))
        out.append(np.concatenate([high, high, low], 1))
    return np.stack(out)


def _channel_table():
    positions = np.arange(QUARTER)[:, None]
    columns = []
    for odd in range(2):
        channels = CH0 + np.arange(odd, CHANNELS, 2)[None, :]
        angles = 2.0 * np.pi * (positions * channels % NFFT) / NFFT
        columns += [np.cos(angles), -np.sin(angles)]
    return _as_bf16(np.concatenate(columns, 1))


def _turn_signs():
    even = np.where(np.arange(0, CHANNELS, 2) % 4 == 0, 1.0, -1.0)
    odd = np.where(np.arange(1, CHANNELS, 2) % 4 == 1, 1.0, -1.0)
    rows = np.concatenate([even, even, odd, -odd])[None, :]
    return _as_bf16(np.broadcast_to(rows, (16, 2 * CHANNELS)))


def _dot(a, b):
    return jnp.dot(a, b, preferred_element_type=F32)


def _split(values):
    high = values.astype(BF16)
    return high, (values - high.astype(F32)).astype(BF16)


def channelize_kernel(x0, x1, x2, x3, c0, c1, c2, c3, table, signs, forward, taps, inverse, own, halo, acc):
    step = pl.program_id(0)

    @pl.when(step == 0)
    def _():
        acc[...] = jnp.zeros_like(acc)

    tap_matrix = taps[...]
    responses = []
    for coefficient in (c0, c1, c2, c3):
        high, low = _split(coefficient[...])
        response = _dot(tap_matrix, jnp.concatenate([high, low, high], 0))
        responses.append((response[:BINS][None], response[BINS:][None]))
    table_even = table[:, : CHANNELS]
    table_odd = table[:, CHANNELS :]
    half = CHANNELS // 2
    turned_even = table_even * signs[0:1, : CHANNELS]
    turned_odd = jnp.concatenate([table_odd[:, half:], table_odd[:, :half]], 1) * signs[0:1, CHANNELS :]
    matrix = forward[...]
    rows = HALF * FRAMES_HERE
    for h in range(2):
        products = []
        for x, (real, imag) in zip((x0, x1, x2, x3), responses):
            z = _dot(matrix, x[h * rows : (h + 1) * rows, :])
            zr = z[: HALF * BINS].reshape(HALF, BINS, CHUNK)
            zi = z[HALF * BINS :].reshape(HALF, BINS, CHUNK)
            yr = (zr * real - zi * imag).reshape(HALF * BINS, CHUNK)
            yi = (zr * imag + zi * real).reshape(HALF * BINS, CHUNK)
            products.append((yr, yi))
        (r0, i0), (r1, i1), (r2, i2), (r3, i3) = products
        even0 = jnp.concatenate([(r0 + r2).astype(BF16), (i0 + i2).astype(BF16)], 0)
        odd0 = jnp.concatenate([(r0 - r2).astype(BF16), (i0 - i2).astype(BF16)], 0)
        even1 = jnp.concatenate([(r1 + r3).astype(BF16), (i1 + i3).astype(BF16)], 0)
        odd1 = jnp.concatenate([(r1 - r3).astype(BF16), (i1 - i3).astype(BF16)], 0)
        acc[h, :, : CHANNELS] += _dot(even0, table_even) + _dot(even1, turned_even)
        acc[h, :, CHANNELS :] += _dot(odd0, table_odd) + _dot(odd1, turned_odd)

    @pl.when(step == STEPS - 1)
    def _():
        held = None
        for s in (0, 4, 1, 5, 2, 6, 3, 7):
            pieces = []
            for ri in range(2):
                for p in range(2):
                    for part in range(2):
                        start = part * HALF * BINS + s * BINS
                        block = acc[p, start : start + BINS, :]
                        left = ri * half
                        pieces.append(
                            jnp.concatenate(
                                [block[:, left : left + half], block[:, CHANNELS + left : CHANNELS + left + half]], 1
                            )
                        )
            stacked = jnp.concatenate(pieces, 0)
            high, low = _split(stacked)
            result = _dot(inverse[s // 4], jnp.concatenate([high, low, high], 0))
            mine, before = result[:128], result[128:]
            own[pl.ds(s, half, stride=2 * HALF), :] = mine[:, :half].T
            own[pl.ds(HALF + s, half, stride=2 * HALF), :] = mine[:, half:].T
            if s < HALF // 2:
                held = before
            else:
                both = held + before
                j = s - HALF // 2
                halo[pl.ds(j, half, stride=HALF), :] = both[:, :half].T
                halo[pl.ds(HALF // 2 + j, half, stride=HALF), :] = both[:, half:].T


def channelize(samples, coefficients):
    x = samples.reshape(INPUTS_HERE * FRAMES_HERE, NFFT)
    whole = lambda *shape: pl.BlockSpec(shape, lambda j: (0,) * len(shape))
    x_specs = [
        pl.BlockSpec((INPUTS_HERE * FRAMES_HERE, CHUNK), functools.partial(lambda q, j: (0, q * STEPS + j), q))
        for q in range(4)
    ]
    c_specs = [
        pl.BlockSpec((TAPS, CHUNK), functools.partial(lambda q, j: (0, q * STEPS + j), q)) for q in range(4)
    ]
    table, signs = _channel_table(), _turn_signs()
    forward, taps, inverse = _as_bf16(_forward_matrix()), _tap_matrix(), _inverse_matrices()
    return pl.pallas_call(
        channelize_kernel,
        out_shape=(
            jax.ShapeDtypeStruct((CHANNELS * HALF, 128), F32),
            jax.ShapeDtypeStruct((CHANNELS * HALF // 2, 128), F32),
        ),
        grid=(STEPS,),
        in_specs=x_specs
        + c_specs
        + [
            pl.BlockSpec((CHUNK, 2 * CHANNELS), lambda j: (j, 0)),
            whole(*signs.shape),
            whole(*forward.shape),
            whole(*taps.shape),
            whole(*inverse.shape),
        ],
        out_specs=(whole(CHANNELS * HALF, 128), whole(CHANNELS * HALF // 2, 128)),
        scratch_shapes=[pltpu.VMEM((2, 2 * HALF * BINS, 2 * CHANNELS), F32)],
        name="channelize",
    )(x, x, x, x, coefficients, coefficients, coefficients, coefficients, table, signs, forward, taps, inverse)


def exchange_kernel(
    own, halo, out, message, total, leaving, arrived, wide, local_sem, halo_send, halo_recv, send_sem, recv_sem
):
    st = lax.axis_index("st")
    ta = lax.axis_index("ta")
    ta_count = 4
    count = CHANNELS
    me = st * ta_count + ta
    barrier = pltpu.get_barrier_semaphore()

    def greet(d, carry):
        peer = lax.rem(me + d, count)
        pl.semaphore_signal(
            barrier, inc=1, device_id=(peer // ta_count, lax.rem(peer, ta_count)), device_id_type=MESH_IDS
        )
        return carry

    lax.fori_loop(1, count, greet, 0)
    leaving[...] = halo[...].astype(BF16)
    pl.semaphore_wait(barrier, count - 1)

    def halo_copy(target):
        return pltpu.make_async_remote_copy(
            src_ref=leaving, dst_ref=arrived, send_sem=halo_send, recv_sem=halo_recv,
            device_id=(st, target), device_id_type=MESH_IDS,
        )

    @pl.when(ta > 0)
    def _():
        halo_copy(ta - 1).start()

    @pl.when(ta == ta_count - 1)
    def _():
        message[...] = own[...].reshape(CHANNELS, HALF, 128).astype(BF16)

    @pl.when(ta < ta_count - 1)
    def _():
        halo_copy(ta).wait_recv()
        wide[...] = arrived[...].astype(F32)
        lane = lax.broadcasted_iota(jnp.int32, (CHANNELS, 128), 1)
        late = lax.rem(lane, FRAMES_HERE) >= FRAMES_HERE // 2
        for s in range(HALF):
            packed = wide[pl.ds(s % 4, CHANNELS, stride=4), :]
            if s >= HALF // 2:
                packed = pltpu.roll(packed, FRAMES_HERE // 2, 1)
            rows = pl.ds(s, CHANNELS, stride=HALF)
            total[rows, :] = own[rows, :] + jnp.where(late, packed, 0.0)
        message[...] = total[...].reshape(CHANNELS, HALF, 128).astype(BF16)

    keep = pltpu.make_async_copy(message.at[me], out.at[me], local_sem)
    keep.start()

    def send(d, carry):
        peer = lax.rem(me + d, count)
        pltpu.make_async_remote_copy(
            src_ref=message.at[peer], dst_ref=out.at[me], send_sem=send_sem, recv_sem=recv_sem,
            device_id=(peer // ta_count, lax.rem(peer, ta_count)), device_id_type=MESH_IDS,
        ).start()
        return carry

    lax.fori_loop(1, count, send, 0)
    keep.wait()

    @pl.when(ta > 0)
    def _():
        halo_copy(ta - 1).wait_send()

    pltpu.make_async_remote_copy(
        src_ref=message.at[pl.ds(0, count - 1)], dst_ref=out.at[pl.ds(0, count - 1)], send_sem=send_sem,
        recv_sem=recv_sem, device_id=(st, ta), device_id_type=MESH_IDS,
    ).wait()


def exchange(own, halo):
    vmem = pl.BlockSpec(memory_space=pltpu.VMEM)
    return pl.pallas_call(
        exchange_kernel,
        out_shape=jax.ShapeDtypeStruct((CHANNELS, HALF, 128), BF16),
        in_specs=[vmem, vmem],
        out_specs=vmem,
        scratch_shapes=[
            pltpu.VMEM((CHANNELS, HALF, 128), BF16),
            pltpu.VMEM((CHANNELS * HALF, 128), F32),
            pltpu.VMEM((CHANNELS * HALF // 2, 128), BF16),
            pltpu.VMEM((CHANNELS * HALF // 2, 128), BF16),
            pltpu.VMEM((CHANNELS * HALF // 2, 128), F32),
        ]
        + [pltpu.SemaphoreType.DMA] * 5,
        compiler_params=pltpu.CompilerParams(collective_id=0, has_side_effects=True),
        name="exchange",
    )(own, halo)


ROWS = 256


def correlate_kernel(arrived, out, spectra):
    inputs = spectra.shape[0]
    step = pl.program_id(0)

    @pl.when(step == 0)
    def _():
        lane = lax.broadcasted_iota(jnp.int32, (8, 8, 128), 2) // FRAMES_HERE

        def place(b, carry):
            tiles = arrived[pl.ds(b * 32, 32)].astype(F32).reshape(8, 4, 8, 128)
            for p in range(2):
                for ri in range(2):
                    g = 2 * p + ri
                    made = None
                    for ta in range(4):
                        turned = tiles[:, ta]
                        if ta != g:
                            turned = pltpu.roll(turned, (ta - g) % 4 * FRAMES_HERE, 2)
                        made = turned if made is None else jnp.where(lane == ta, turned, made)
                    for k in range(8):
                        start = pl.multiple_of(b * 128 + k * 16 + p * 8, 8)
                        wide_rows = made[k]
                        spectra[pl.ds(start, 8), ri * 128 : (ri + 1) * 128] = wide_rows
            return carry

        lax.fori_loop(0, inputs // 128, place, 0)

    start = pl.multiple_of(step * ROWS, ROWS)
    block = spectra[pl.ds(start, ROWS), :].astype(BF16)
    everything = spectra[...].astype(BF16)
    contract = (((1,), (1,)), ((), ()))
    swapped = jnp.concatenate([block[:, 128:], -block[:, :128]], 1)
    scale = 1.0 / 128
    out[0, 0] = (lax.dot_general(block, everything, contract, preferred_element_type=F32) * scale).astype(BF16)
    out[0, 1] = (lax.dot_general(swapped, everything, contract, preferred_element_type=F32) * scale).astype(BF16)


def correlate(arrived):
    inputs = arrived.shape[0] // 4 * INPUTS_HERE
    return pl.pallas_call(
        correlate_kernel,
        out_shape=jax.ShapeDtypeStruct((1, 2, inputs, inputs), BF16),
        grid=(inputs // ROWS,),
        in_specs=[pl.BlockSpec(arrived.shape, lambda i: (0, 0, 0))],
        out_specs=pl.BlockSpec((1, 2, ROWS, inputs), lambda i: (0, 0, i, 0)),
        scratch_shapes=[pltpu.VMEM((inputs, 256), F32)],
        name="correlate",
    )(arrived)


def on_device(samples, coefficients):
    own, halo = channelize(samples, coefficients)
    return correlate(exchange(own, halo))


def solution(mesh):
    return jax.shard_map(
        on_device,
        mesh=mesh,
        in_specs=(P("st", "ta", None), P()),
        out_specs=P(("st", "ta"), None, None, None),
        check_vma=False,
    )
```

```python
import functools
import math

import jax
import jax.numpy as jnp
import numpy as np
from jax import lax
from jax.experimental import pallas as pl
from jax.experimental.pallas import tpu as pltpu
from jax.sharding import PartitionSpec as P

CH0 = 1024
LOGICAL = pl.DeviceIdType.LOGICAL
BF16 = jnp.bfloat16
F32 = jnp.float32

NFFT = 8192
TAPS = 16
INPUTS_HERE = 16
FRAMES_HERE = 32
CHANNELS = 256
TA = 4
BINS = 24
HALF = 8
GROUPS = 4
HALF_FRAMES = FRAMES_HERE // 2
QUARTER = NFFT // 4
CHUNK = 256
STEPS = QUARTER // CHUNK


def _as_bf16(values):
    return np.asarray(values, np.float32).astype(BF16)


def _high_low(values):
    high = _as_bf16(values)
    return high, _as_bf16(values - high.astype(np.float64))


def _bin_angles():
    return 2.0 * np.pi * (np.arange(BINS) + 0.5) / (2 * BINS)


def _forward_matrix():
    angles = _bin_angles()[:, None] * np.arange(FRAMES_HERE)[None, :]
    parts = np.stack([np.cos(angles), -np.sin(angles)])
    block = np.zeros((2, HALF, BINS, HALF, FRAMES_HERE))
    for i in range(HALF):
        block[:, i, :, i, :] = parts
    return block.reshape(2 * HALF * BINS, HALF * FRAMES_HERE)


def _tap_matrix():
    angles = _bin_angles()[:, None] * np.arange(TAPS)[None, :]
    taps = np.concatenate([np.cos(angles), np.sin(angles)])
    high, low = _high_low(taps)
    return np.concatenate([high, high, low], 1)


def _inverse_matrix():
    scale = (2.0 / (2 * BINS)) * NFFT ** -0.5
    rows = np.zeros((3, GROUPS, 2, HALF_FRAMES, 2, GROUPS, 2, BINS))
    for kind, first in enumerate((0, HALF_FRAMES, -HALF_FRAMES)):
        frames = first + np.arange(HALF_FRAMES)
        angles = _bin_angles()[:, None] * frames[None, :]
        values = scale * np.stack([np.cos(angles), -np.sin(angles)])
        if first < 0:
            values[:, :, frames <= -TAPS] = 0.0
        for p in range(GROUPS):
            for ri in range(2):
                rows[kind, p, ri, :, ri, p] = np.moveaxis(values, 2, 0)
    high, low = _high_low(rows.reshape(3 * 128, 4 * GROUPS * BINS))
    return np.concatenate([high, high, low], 1)


def _channel_table():
    positions = np.arange(QUARTER)[:, None]
    columns = []
    for odd in range(2):
        channels = CH0 + np.arange(odd, CHANNELS, 2)[None, :]
        angles = 2.0 * np.pi * (positions * channels % NFFT) / NFFT
        columns += [np.cos(angles), -np.sin(angles)]
    return _as_bf16(np.concatenate(columns, 1))


def _turn_signs():
    even = np.where(np.arange(0, CHANNELS, 2) % 4 == 0, 1.0, -1.0)
    odd = np.where(np.arange(1, CHANNELS, 2) % 4 == 1, 1.0, -1.0)
    rows = np.concatenate([even, even, odd, -odd])[None, :]
    return _as_bf16(np.broadcast_to(rows, (16, 2 * CHANNELS)))


def _dot(a, b):
    return jnp.dot(a, b, preferred_element_type=F32)


def _split(values):
    high = values.astype(BF16)
    return high, (values - high.astype(F32)).astype(BF16)


def spectra_kernel(
    x0, x1, x2, x3, c0, c1, c2, c3, table, signs, forward, taps, inverse,
    out,
    acc, own, halo, early, late, leaving, arrived, wide, local_sem, halo_send, halo_recv, send_sem, recv_sem,
):
    step = pl.program_id(0)
    st = lax.axis_index("st")
    ta = lax.axis_index("ta")
    me = st * TA + ta
    barrier = pltpu.get_barrier_semaphore()

    def over_others(body):
        def run(peer, carry):
            body(peer)
            return carry

        lax.fori_loop(me + 1, CHANNELS, run, 0)
        lax.fori_loop(0, me, run, 0)

    @pl.when(step == 0)
    def _():
        over_others(lambda peer: pl.semaphore_signal(barrier, inc=1, device_id=peer, device_id_type=LOGICAL))
        acc[...] = jnp.zeros_like(acc)

    tap_matrix = taps[...]
    responses = []
    for coefficient in (c0, c1, c2, c3):
        high, low = _split(coefficient[...])
        response = _dot(tap_matrix, jnp.concatenate([high, low, high], 0))
        responses.append((response[:BINS][None], response[BINS:][None]))
    table_even = table[:, : CHANNELS]
    table_odd = table[:, CHANNELS :]
    half = CHANNELS // 2
    turned_even = table_even * signs[0:1, : CHANNELS]
    turned_odd = jnp.concatenate([table_odd[:, half:], table_odd[:, :half]], 1) * signs[0:1, CHANNELS :]
    matrix = forward[...]
    rows = HALF * FRAMES_HERE
    for h in range(2):
        products = []
        for x, (real, imag) in zip((x0, x1, x2, x3), responses):
            z = _dot(matrix, x[h * rows : (h + 1) * rows, :])
            zr = z[: HALF * BINS].reshape(HALF, BINS, CHUNK)
            zi = z[HALF * BINS :].reshape(HALF, BINS, CHUNK)
            yr = (zr * real - zi * imag).reshape(HALF * BINS, CHUNK)
            yi = (zr * imag + zi * real).reshape(HALF * BINS, CHUNK)
            products.append((yr, yi))
        (r0, i0), (r1, i1), (r2, i2), (r3, i3) = products
        even0 = jnp.concatenate([(r0 + r2).astype(BF16), (i0 + i2).astype(BF16)], 0)
        odd0 = jnp.concatenate([(r0 - r2).astype(BF16), (i0 - i2).astype(BF16)], 0)
        even1 = jnp.concatenate([(r1 + r3).astype(BF16), (i1 + i3).astype(BF16)], 0)
        odd1 = jnp.concatenate([(r1 - r3).astype(BF16), (i1 - i3).astype(BF16)], 0)
        acc[h, :, : CHANNELS] += _dot(even0, table_even) + _dot(even1, turned_even)
        acc[h, :, CHANNELS :] += _dot(odd0, table_odd) + _dot(odd1, turned_odd)

    def transform_back():
        for s in range(HALF // 2):
            pieces = []
            for ri in range(2):
                left = ri * half
                for p in range(GROUPS):
                    for part in range(2):
                        start = part * HALF * BINS + (p % 2 * 4 + s) * BINS
                        block = acc[p // 2, start : start + BINS, :]
                        pieces.append(
                            jnp.concatenate(
                                [block[:, left : left + half], block[:, CHANNELS + left : CHANNELS + left + half]], 1
                            )
                        )
            high, low = _split(jnp.concatenate(pieces, 0))
            result = _dot(inverse[...], jnp.concatenate([high, low, high], 0))
            for odd in range(2):
                columns = slice(odd * half, (odd + 1) * half)
                own[pl.ds(odd * 8 + s, half, stride=16), :] = result[:128, columns].T
                own[pl.ds(odd * 8 + 4 + s, half, stride=16), :] = result[128:256, columns].T
                halo[pl.ds(odd * 4 + s, half, stride=8), :] = result[256:, columns].T

    def halo_copy(target):
        return pltpu.make_async_remote_copy(
            src_ref=leaving, dst_ref=arrived, send_sem=halo_send, recv_sem=halo_recv,
            device_id=st * TA + target, device_id_type=LOGICAL,
        )

    def part_copies(message, first):
        rows = pl.ds(first, 4)

        def send(peer):
            pltpu.make_async_remote_copy(
                src_ref=message.at[peer, rows], dst_ref=out.at[me, rows], send_sem=send_sem, recv_sem=recv_sem,
                device_id=peer, device_id_type=LOGICAL,
            ).start()

        keep = pltpu.make_async_copy(message.at[me, rows], out.at[me, rows], local_sem.at[first // 4])
        keep.start()
        over_others(send)
        return keep

    @pl.when(step == STEPS - 1)
    def _():
        transform_back()
        leaving[...] = halo[...].astype(BF16)
        early[...] = own[...].reshape(CHANNELS, HALF, 128).astype(BF16)
        pl.semaphore_wait(barrier, CHANNELS - 1)

        @pl.when(ta > 0)
        def _():
            halo_copy(ta - 1).start()

        keep_early = part_copies(early, 0)

        @pl.when(ta < TA - 1)
        def _():
            halo_copy(ta).wait_recv()
            wide[...] = arrived[...].astype(F32)
            for s in range(4):
                rows = pl.ds(4 + s, CHANNELS, stride=HALF)
                own[rows, :] += wide[pl.ds(s, CHANNELS, stride=4), :]

        late[...] = own[...].reshape(CHANNELS, HALF, 128).astype(BF16)
        keep_late = part_copies(late, 4)
        keep_early.wait()
        keep_late.wait()

        @pl.when(ta > 0)
        def _():
            halo_copy(ta - 1).wait_send()

        everything = pl.ds(0, CHANNELS - 1)
        pltpu.make_async_remote_copy(
            src_ref=late.at[everything], dst_ref=out.at[everything], send_sem=send_sem, recv_sem=recv_sem,
            device_id=me, device_id_type=LOGICAL,
        ).wait()


def gather_spectra(samples, coefficients):
    x = samples.reshape(INPUTS_HERE * FRAMES_HERE, NFFT)
    whole = lambda *shape: pl.BlockSpec(shape, lambda j: (0,) * len(shape))
    x_specs = [
        pl.BlockSpec((INPUTS_HERE * FRAMES_HERE, CHUNK), functools.partial(lambda q, j: (0, q * STEPS + j), q))
        for q in range(4)
    ]
    c_specs = [
        pl.BlockSpec((TAPS, CHUNK), functools.partial(lambda q, j: (0, q * STEPS + j), q)) for q in range(4)
    ]
    table, signs = _channel_table(), _turn_signs()
    forward, taps, inverse = _as_bf16(_forward_matrix()), _tap_matrix(), _inverse_matrix()
    rows = CHANNELS * HALF
    return pl.pallas_call(
        spectra_kernel,
        out_shape=jax.ShapeDtypeStruct((CHANNELS, HALF, 128), BF16),
        grid=(STEPS,),
        in_specs=x_specs
        + c_specs
        + [
            pl.BlockSpec((CHUNK, 2 * CHANNELS), lambda j: (j, 0)),
            whole(*signs.shape),
            whole(*forward.shape),
            whole(*taps.shape),
            whole(*inverse.shape),
        ],
        out_specs=pl.BlockSpec(memory_space=pl.ANY),
        scratch_shapes=[
            pltpu.VMEM((2, 2 * HALF * BINS, 2 * CHANNELS), F32),
            pltpu.VMEM((rows, 128), F32),
            pltpu.VMEM((rows // 2, 128), F32),
            pltpu.VMEM((CHANNELS, HALF, 128), BF16),
            pltpu.VMEM((CHANNELS, HALF, 128), BF16),
            pltpu.VMEM((rows // 2, 128), BF16),
            pltpu.VMEM((rows // 2, 128), BF16),
            pltpu.VMEM((rows // 2, 128), F32),
            pltpu.SemaphoreType.DMA((2,)),
        ]
        + [pltpu.SemaphoreType.DMA] * 4,
        compiler_params=pltpu.CompilerParams(collective_id=0, has_side_effects=True),
        name="spectra",
    )(x, x, x, x, coefficients, coefficients, coefficients, coefficients, table, signs, forward, taps, inverse)


ROWS = 256


def correlate_kernel(arrived, out, spectra, wide):
    inputs = spectra.shape[1]
    step = pl.program_id(0)

    @pl.when(step == 0)
    def _():
        wide[...] = arrived[...].astype(F32).reshape(wide.shape)
        sources = inputs // INPUTS_HERE
        lane = lax.broadcasted_iota(jnp.int32, (sources, 128), 1) // HALF_FRAMES
        for s in range(4):
            tiles = [wide[pl.ds(4 * t + s, sources, stride=32), :] for t in range(8)]
            for bit in (1, 2, 4):
                shift = bit * HALF_FRAMES
                low = lane // bit % 2 == 0
                for t in range(8):
                    if t & bit == 0:
                        a, b = tiles[t], tiles[t + bit]
                        tiles[t] = jnp.where(low, a, pltpu.roll(b, shift, 1))
                        tiles[t + bit] = jnp.where(low, pltpu.roll(a, 128 - shift, 1), b)
            for p in range(GROUPS):
                for ri in range(2):
                    spectra[ri, pl.ds(p * 4 + s, sources, stride=INPUTS_HERE), :] = tiles[2 * p + ri]

    start = pl.multiple_of(step * ROWS, ROWS)
    real = spectra[0, pl.ds(start, ROWS), :].astype(BF16)
    imag = spectra[1, pl.ds(start, ROWS), :].astype(BF16)
    block = jnp.concatenate([real, imag], 1)
    swapped = jnp.concatenate([imag, -real], 1)
    everything = jnp.concatenate([spectra[0].astype(BF16), spectra[1].astype(BF16)], 1)
    contract = (((1,), (1,)), ((), ()))
    scale = 1.0 / 128
    out[0, 0] = (lax.dot_general(block, everything, contract, preferred_element_type=F32) * scale).astype(BF16)
    out[0, 1] = (lax.dot_general(swapped, everything, contract, preferred_element_type=F32) * scale).astype(BF16)


def correlate(arrived):
    inputs = arrived.shape[0] // 4 * INPUTS_HERE
    return pl.pallas_call(
        correlate_kernel,
        out_shape=jax.ShapeDtypeStruct((1, 2, inputs, inputs), BF16),
        grid=(inputs // ROWS,),
        in_specs=[pl.BlockSpec(arrived.shape, lambda i: (0, 0, 0))],
        out_specs=pl.BlockSpec((1, 2, ROWS, inputs), lambda i: (0, 0, i, 0)),
        scratch_shapes=[pltpu.VMEM((2, inputs, 128), F32), pltpu.VMEM((arrived.shape[0] * 8, 128), F32)],
        name="correlate",
    )(arrived)


def on_device(samples, coefficients):
    return correlate(gather_spectra(samples, coefficients))


def solution(mesh):
    return jax.shard_map(
        on_device,
        mesh=mesh,
        in_specs=(P("st", "ta", None), P()),
        out_specs=P(("st", "ta"), None, None, None),
        check_vma=False,
    )
```

```python
import functools
import math

import jax
import jax.numpy as jnp
import numpy as np
from jax import lax
from jax.experimental import pallas as pl
from jax.experimental.pallas import tpu as pltpu
from jax.sharding import PartitionSpec as P

CH0 = 1024
LOGICAL = pl.DeviceIdType.LOGICAL
BF16 = jnp.bfloat16
F32 = jnp.float32

NFFT = 8192
TAPS = 16
INPUTS_HERE = 16
FRAMES_HERE = 32
CHANNELS = 256
TA = 4
BINS = 24
HALF = 8
GROUPS = 4
HALF_FRAMES = FRAMES_HERE // 2
QUARTER = NFFT // 4
CHUNK = 256
STEPS = QUARTER // CHUNK


def _as_bf16(values):
    return np.asarray(values, np.float32).astype(BF16)


def _high_low(values):
    high = _as_bf16(values)
    return high, _as_bf16(values - high.astype(np.float64))


def _bin_angles():
    return 2.0 * np.pi * (np.arange(BINS) + 0.5) / (2 * BINS)


def _forward_matrix():
    angles = _bin_angles()[:, None] * np.arange(FRAMES_HERE)[None, :]
    parts = np.stack([np.cos(angles), -np.sin(angles)])
    block = np.zeros((HALF, 2, BINS, HALF, FRAMES_HERE))
    for i in range(HALF):
        block[i, :, :, i, :] = parts
    return block.reshape(2 * HALF * BINS, HALF * FRAMES_HERE)


def _tap_matrix():
    angles = _bin_angles()[:, None] * np.arange(TAPS)[None, :]
    taps = np.concatenate([np.cos(angles), np.sin(angles)])
    high, low = _high_low(taps)
    return np.concatenate([high, high, low], 1)


def _inverse_matrix():
    scale = (2.0 / (2 * BINS)) * NFFT ** -0.5
    rows = np.zeros((3, GROUPS, HALF_FRAMES, GROUPS, 2, BINS))
    for kind, first in enumerate((0, HALF_FRAMES, -HALF_FRAMES)):
        frames = first + np.arange(HALF_FRAMES)
        angles = _bin_angles()[:, None] * frames[None, :]
        values = scale * np.stack([np.cos(angles), -np.sin(angles)])
        if first < 0:
            values[:, :, frames <= -TAPS] = 0.0
        for p in range(GROUPS):
            rows[kind, p, :, p] = np.moveaxis(values, 2, 0)
    high, low = _high_low(rows.reshape(3 * GROUPS * HALF_FRAMES, 2 * GROUPS * BINS))
    return np.concatenate([high, high, low], 1)


def _channel_table():
    positions = np.arange(QUARTER)[:, None]
    columns = []
    for odd in range(2):
        channels = CH0 + np.arange(odd, CHANNELS, 2)[None, :]
        angles = 2.0 * np.pi * (positions * channels % NFFT) / NFFT
        columns += [np.cos(angles), -np.sin(angles)]
    return _as_bf16(np.concatenate(columns, 1))


def _turn_signs():
    even = np.where(np.arange(0, CHANNELS, 2) % 4 == 0, 1.0, -1.0)
    odd = np.where(np.arange(1, CHANNELS, 2) % 4 == 1, 1.0, -1.0)
    rows = np.concatenate([even, even, odd, -odd])[None, :]
    return _as_bf16(np.broadcast_to(rows, (16, 2 * CHANNELS)))


def _dot(a, b):
    return jnp.dot(a, b, preferred_element_type=F32)


def _split(values):
    high = values.astype(BF16)
    return high, (values - high.astype(F32)).astype(BF16)


def spectra_kernel(
    x, coefficients, table_all, inverse_all, signs, forward, taps,
    out,
    x_slots, c_slots, table_slots, inverse, in_sems, inverse_sem, acc, own, halo, early, late, leaving, arrived, wide, local_sem, halo_send, halo_recv, send_sem, recv_sem,
):
    step = pl.program_id(0)
    st = lax.axis_index("st")
    ta = lax.axis_index("ta")
    me = st * TA + ta
    barrier = pltpu.get_barrier_semaphore()

    def over_others(body):
        def run(peer, carry):
            body(peer)
            return carry

        lax.fori_loop(me + 1, CHANNELS, run, 0)
        lax.fori_loop(0, me, run, 0)

    def inputs(j):
        slot = lax.rem(j, 2)
        copies = []
        for q in range(4):
            columns = pl.ds(pl.multiple_of((q * STEPS + j) * CHUNK, CHUNK), CHUNK)
            copies.append(pltpu.make_async_copy(x.at[:, columns], x_slots.at[slot, q], in_sems.at[slot, q]))
            copies.append(
                pltpu.make_async_copy(coefficients.at[:, columns], c_slots.at[slot, q], in_sems.at[slot, 4 + q])
            )
        lines = pl.ds(pl.multiple_of(j * CHUNK, CHUNK), CHUNK)
        copies.append(pltpu.make_async_copy(table_all.at[lines], table_slots.at[slot], in_sems.at[slot, 8]))
        return copies

    inverse_copy = pltpu.make_async_copy(inverse_all, inverse, inverse_sem)

    @pl.when(step == 0)
    def _():
        for copy in inputs(step):
            copy.start()
        inverse_copy.start()
        over_others(lambda peer: pl.semaphore_signal(barrier, inc=1, device_id=peer, device_id_type=LOGICAL))
        acc[...] = jnp.zeros_like(acc)

    @pl.when(step < STEPS - 1)
    def _():
        for copy in inputs(step + 1):
            copy.start()

    for copy in inputs(step):
        copy.wait()
    slot = lax.rem(step, 2)
    table = table_slots[slot]
    tap_matrix = taps[...]
    responses = []
    for q in range(4):
        high, low = _split(c_slots[slot, q])
        response = _dot(tap_matrix, jnp.concatenate([high, low, high], 0))
        responses.append((response[:BINS][None], response[BINS:][None]))
    table_even = table[:, : CHANNELS]
    table_odd = table[:, CHANNELS :]
    half = CHANNELS // 2
    turned_even = table_even * signs[0:1, : CHANNELS]
    turned_odd = jnp.concatenate([table_odd[:, half:], table_odd[:, :half]], 1) * signs[0:1, CHANNELS :]
    matrix = forward[...]
    rows = HALF * FRAMES_HERE
    weights_even = jnp.concatenate([table_even, turned_even], 0)
    weights_odd = jnp.concatenate([table_odd, turned_odd], 0)

    def product(q, h):
        real, imag = responses[q]
        z = _dot(matrix, x_slots[slot, q, h * rows : (h + 1) * rows, :]).reshape(HALF, 2, BINS, CHUNK)
        zr, zi = z[:, 0], z[:, 1]
        return zr * real - zi * imag, zr * imag + zi * real

    def joined(r, i):
        return jnp.stack([r, i], 1).reshape(2 * HALF * BINS, CHUNK).astype(BF16)

    for h in range(2):
        evens, odds = [], []
        for q in range(2):
            (ra, ia), (rb, ib) = product(q, h), product(q + 2, h)
            evens.append(joined(ra + rb, ia + ib))
            odds.append(joined(ra - rb, ia - ib))
        acc[h, :, : CHANNELS] += _dot(jnp.concatenate(evens, 1), weights_even)
        acc[h, :, CHANNELS :] += _dot(jnp.concatenate(odds, 1), weights_odd)

    def transform_back():
        for s in range(HALF // 2):
            results = []
            for ri in range(2):
                left = ri * half
                blocks = []
                for p in range(GROUPS):
                    start = (p % 2 * 4 + s) * 2 * BINS
                    block = acc[p // 2, start : start + 2 * BINS, :]
                    blocks.append(
                        jnp.concatenate(
                            [block[:, left : left + half], block[:, CHANNELS + left : CHANNELS + left + half]], 1
                        )
                    )
                high, low = _split(jnp.concatenate(blocks, 0))
                results.append(_dot(inverse[...], jnp.concatenate([high, low, high], 0)))
            for odd in range(2):
                columns = slice(odd * half, (odd + 1) * half)

                def turned(kind):
                    lines = slice(kind * 64, (kind + 1) * 64)
                    return jnp.concatenate([results[0][lines, columns], results[1][lines, columns]], 0).T

                own[pl.ds(odd * 8 + s, half, stride=16), :] = turned(0)
                own[pl.ds(odd * 8 + 4 + s, half, stride=16), :] = turned(1)
                halo[pl.ds(odd * 4 + s, half, stride=8), :] = turned(2)

    def halo_copy(target):
        return pltpu.make_async_remote_copy(
            src_ref=leaving, dst_ref=arrived, send_sem=halo_send, recv_sem=halo_recv,
            device_id=st * TA + target, device_id_type=LOGICAL,
        )

    def part_copies(message, first):
        rows = pl.ds(first, 4)

        def send(peer):
            pltpu.make_async_remote_copy(
                src_ref=message.at[peer, rows], dst_ref=out.at[me, rows], send_sem=send_sem, recv_sem=recv_sem,
                device_id=peer, device_id_type=LOGICAL,
            ).start()

        keep = pltpu.make_async_copy(message.at[me, rows], out.at[me, rows], local_sem.at[first // 4])
        keep.start()
        over_others(send)
        return keep

    @pl.when(step == STEPS - 1)
    def _():
        inverse_copy.wait()
        transform_back()
        leaving[...] = halo[...].astype(BF16)
        early[...] = own[...].reshape(CHANNELS, HALF, 128).astype(BF16)
        pl.semaphore_wait(barrier, CHANNELS - 1)

        @pl.when(ta > 0)
        def _():
            halo_copy(ta - 1).start()

        keep_early = part_copies(early, 0)

        @pl.when(ta < TA - 1)
        def _():
            halo_copy(ta).wait_recv()
            wide[...] = arrived[...].astype(F32)
            for s in range(4):
                rows = pl.ds(4 + s, CHANNELS, stride=HALF)
                own[rows, :] += wide[pl.ds(s, CHANNELS, stride=4), :]

        late[...] = own[...].reshape(CHANNELS, HALF, 128).astype(BF16)
        keep_late = part_copies(late, 4)
        keep_early.wait()
        keep_late.wait()

        @pl.when(ta > 0)
        def _():
            halo_copy(ta - 1).wait_send()

        everything = pl.ds(0, CHANNELS - 1)
        pltpu.make_async_remote_copy(
            src_ref=late.at[everything], dst_ref=out.at[everything], send_sem=send_sem, recv_sem=recv_sem,
            device_id=me, device_id_type=LOGICAL,
        ).wait()


def gather_spectra(samples, coefficients):
    x = samples.reshape(INPUTS_HERE * FRAMES_HERE, NFFT)
    whole = lambda *shape: pl.BlockSpec(shape, lambda j: (0,) * len(shape))
    left = pl.BlockSpec(memory_space=pl.ANY)
    table, signs = _channel_table(), _turn_signs()
    forward, taps, inverse = _as_bf16(_forward_matrix()), _tap_matrix(), _inverse_matrix()
    rows = CHANNELS * HALF
    return pl.pallas_call(
        spectra_kernel,
        out_shape=jax.ShapeDtypeStruct((CHANNELS, HALF, 128), BF16),
        grid=(STEPS,),
        in_specs=[left, left, left, left, whole(*signs.shape), whole(*forward.shape), whole(*taps.shape)],
        out_specs=pl.BlockSpec(memory_space=pl.ANY),
        scratch_shapes=[
            pltpu.VMEM((2, 4, INPUTS_HERE * FRAMES_HERE, CHUNK), BF16),
            pltpu.VMEM((2, 4, TAPS, CHUNK), F32),
            pltpu.VMEM((2, CHUNK, 2 * CHANNELS), BF16),
            pltpu.VMEM(inverse.shape, BF16),
            pltpu.SemaphoreType.DMA((2, 9)),
            pltpu.SemaphoreType.DMA,
            pltpu.VMEM((2, 2 * HALF * BINS, 2 * CHANNELS), F32),
            pltpu.VMEM((rows, 128), F32),
            pltpu.VMEM((rows // 2, 128), F32),
            pltpu.VMEM((CHANNELS, HALF, 128), BF16),
            pltpu.VMEM((CHANNELS, HALF, 128), BF16),
            pltpu.VMEM((rows // 2, 128), BF16),
            pltpu.VMEM((rows // 2, 128), BF16),
            pltpu.VMEM((rows // 2, 128), F32),
            pltpu.SemaphoreType.DMA((2,)),
        ]
        + [pltpu.SemaphoreType.DMA] * 4,
        compiler_params=pltpu.CompilerParams(collective_id=0, has_side_effects=True),
        name="spectra",
    )(x, coefficients, table, inverse, signs, forward, taps)


ROWS = 256


def correlate_kernel(arrived, out, spectra, packed):
    stations = spectra.shape[1]
    step = pl.program_id(0)
    block = ROWS // INPUTS_HERE

    @pl.when(step == 0)
    def _():
        group = lax.broadcasted_iota(jnp.int32, (block, 8, 128), 2) // HALF_FRAMES

        def place(b, carry):
            start = pl.multiple_of(b * block, block)
            lines = arrived[pl.ds(start * TA, block * TA)].astype(F32).reshape(block, TA, 8, 128)
            tiles = [lines[:, t] for t in range(TA)]
            for bit in (1, 2):
                shift = bit * HALF_FRAMES
                low = group // bit % 2 == 0
                for t in range(TA):
                    if t & bit == 0:
                        first, second = tiles[t], tiles[t + bit]
                        tiles[t] = jnp.where(low, first, pltpu.roll(second, shift, 2))
                        tiles[t + bit] = jnp.where(low, pltpu.roll(first, 128 - shift, 2), second)
            for p in range(GROUPS):
                for late in range(2):
                    spectra[late, pl.ds(start, block), p * 4 : (p + 1) * 4, :] = tiles[p][:, late * 4 : late * 4 + 4]
            for late in range(2):
                rows = pl.ds(pl.multiple_of(b * ROWS, ROWS), ROWS)
                values = spectra[late, pl.ds(start, block)].reshape(ROWS, 128)
                packed[rows, late * 128 : (late + 1) * 128] = values.astype(BF16)
            return carry

        lax.fori_loop(0, stations // block, place, 0)

    here = pl.ds(pl.multiple_of(step * block, block), block)
    sign = jnp.where(lax.broadcasted_iota(jnp.int32, (1, 128), 1) < 64, 1.0, -1.0)
    direct, swapped = [], []
    for late in range(2):
        values = spectra[late, here].reshape(ROWS, 128)
        direct.append(values.astype(BF16))
        swapped.append((pltpu.roll(values, 64, 1) * sign).astype(BF16))
    lines = jnp.concatenate([jnp.concatenate(direct, 1), jnp.concatenate(swapped, 1)], 0)
    result = lax.dot_general(lines, packed[...], (((1,), (1,)), ((), ())), preferred_element_type=F32)
    scaled = (result * (1.0 / 128)).astype(BF16)
    out[0, 0] = scaled[:ROWS]
    out[0, 1] = scaled[ROWS:]


def correlate(arrived):
    inputs = arrived.shape[0] // TA * INPUTS_HERE
    return pl.pallas_call(
        correlate_kernel,
        out_shape=jax.ShapeDtypeStruct((1, 2, inputs, inputs), BF16),
        grid=(inputs // ROWS,),
        in_specs=[pl.BlockSpec(arrived.shape, lambda i: (0, 0, 0))],
        out_specs=pl.BlockSpec((1, 2, ROWS, inputs), lambda i: (0, 0, i, 0)),
        scratch_shapes=[
            pltpu.VMEM((2, inputs // INPUTS_HERE, INPUTS_HERE, 128), F32),
            pltpu.VMEM((inputs, 256), BF16),
        ],
        name="correlate",
    )(arrived)


def on_device(samples, coefficients):
    return correlate(gather_spectra(samples, coefficients))


def solution(mesh):
    return jax.shard_map(
        on_device,
        mesh=mesh,
        in_specs=(P("st", "ta", None), P()),
        out_specs=P(("st", "ta"), None, None, None),
        check_vma=False,
    )
```

```python
import functools
import math

import jax
import jax.numpy as jnp
import numpy as np
from jax import lax
from jax.experimental import pallas as pl
from jax.experimental.pallas import tpu as pltpu
from jax.sharding import PartitionSpec as P

CH0 = 1024
LOGICAL = pl.DeviceIdType.LOGICAL
BF16 = jnp.bfloat16
F32 = jnp.float32

NFFT = 8192
TAPS = 16
INPUTS_HERE = 16
FRAMES_HERE = 32
CHANNELS = 256
TA = 4
BINS = 24
HALF = 8
GROUPS = 4
HALF_FRAMES = FRAMES_HERE // 2
QUARTER = NFFT // 4
CHUNK = 512
STEPS = QUARTER // CHUNK


def _as_bf16(values):
    return np.asarray(values, np.float32).astype(BF16)


def _high_low(values):
    high = _as_bf16(values)
    return high, _as_bf16(values - high.astype(np.float64))


def _bin_angles():
    return 2.0 * np.pi * (np.arange(BINS) + 0.5) / (2 * BINS)


def _forward_matrix():
    angles = _bin_angles()[:, None] * np.arange(FRAMES_HERE)[None, :]
    parts = np.stack([np.cos(angles), -np.sin(angles)])
    block = np.zeros((HALF, 2, BINS, HALF, FRAMES_HERE))
    for i in range(HALF):
        block[i, :, :, i, :] = parts
    return block.reshape(2 * HALF * BINS, HALF * FRAMES_HERE)


def _tap_matrix():
    angles = _bin_angles()[:, None] * np.arange(TAPS)[None, :]
    taps = np.concatenate([np.cos(angles), np.sin(angles)])
    high, low = _high_low(taps)
    return np.concatenate([high, high, low], 1)


def _inverse_matrix():
    scale = (2.0 / (2 * BINS)) * NFFT ** -0.5
    rows = np.zeros((3, GROUPS, HALF_FRAMES, GROUPS, 2, BINS))
    for kind, first in enumerate((0, HALF_FRAMES, -HALF_FRAMES)):
        frames = first + np.arange(HALF_FRAMES)
        angles = _bin_angles()[:, None] * frames[None, :]
        values = scale * np.stack([np.cos(angles), -np.sin(angles)])
        if first < 0:
            values[:, :, frames <= -TAPS] = 0.0
        for p in range(GROUPS):
            rows[kind, p, :, p] = np.moveaxis(values, 2, 0)
    high, low = _high_low(rows.reshape(3 * GROUPS * HALF_FRAMES, 2 * GROUPS * BINS))
    return np.concatenate([high, high, low], 1)


def _channel_table():
    positions = np.arange(QUARTER)[:, None]
    columns = []
    for odd in range(2):
        channels = CH0 + np.arange(odd, CHANNELS, 2)[None, :]
        angles = 2.0 * np.pi * (positions * channels % NFFT) / NFFT
        columns += [np.cos(angles), -np.sin(angles)]
    return _as_bf16(np.concatenate(columns, 1))


def _turn_signs():
    even = np.where(np.arange(0, CHANNELS, 2) % 4 == 0, 1.0, -1.0)
    odd = np.where(np.arange(1, CHANNELS, 2) % 4 == 1, 1.0, -1.0)
    rows = np.concatenate([even, even, odd, -odd])[None, :]
    return _as_bf16(np.broadcast_to(rows, (16, 2 * CHANNELS)))


def _dot(a, b):
    return jnp.dot(a, b, preferred_element_type=F32)


def _split(values):
    high = values.astype(BF16)
    return high, (values - high.astype(F32)).astype(BF16)


def spectra_kernel(
    x, coefficients, table_all, inverse_all, signs, forward, taps,
    out,
    x_slots, c_slots, table_slots, inverse, in_sems, inverse_sem, acc, own, halo, early, late, leaving, arrived, wide, local_sem, halo_send, halo_recv, send_sem, recv_sem,
):
    step = pl.program_id(0)
    st = lax.axis_index("st")
    ta = lax.axis_index("ta")
    me = st * TA + ta
    barrier = pltpu.get_barrier_semaphore()

    def over_others(body):
        def run(peer, carry):
            body(peer)
            return carry

        lax.fori_loop(me + 1, CHANNELS, run, 0)
        lax.fori_loop(0, me, run, 0)

    def inputs(j):
        slot = lax.rem(j, 2)
        copies = []
        for q in range(4):
            columns = pl.ds(pl.multiple_of((q * STEPS + j) * CHUNK, CHUNK), CHUNK)
            copies.append(pltpu.make_async_copy(x.at[:, columns], x_slots.at[slot, q], in_sems.at[slot, q]))
            copies.append(
                pltpu.make_async_copy(coefficients.at[:, columns], c_slots.at[slot, q], in_sems.at[slot, 4 + q])
            )
        lines = pl.ds(pl.multiple_of(j * CHUNK, CHUNK), CHUNK)
        copies.append(pltpu.make_async_copy(table_all.at[lines], table_slots.at[slot], in_sems.at[slot, 8]))
        return copies

    inverse_copy = pltpu.make_async_copy(inverse_all, inverse, inverse_sem)

    @pl.when(step == 0)
    def _():
        for copy in inputs(step):
            copy.start()
        inverse_copy.start()
        over_others(lambda peer: pl.semaphore_signal(barrier, inc=1, device_id=peer, device_id_type=LOGICAL))
        acc[...] = jnp.zeros_like(acc)

    @pl.when(step < STEPS - 1)
    def _():
        for copy in inputs(step + 1):
            copy.start()

    for copy in inputs(step):
        copy.wait()
    slot = lax.rem(step, 2)
    table = table_slots[slot]
    tap_matrix = taps[...]
    responses = []
    for q in range(4):
        high, low = _split(c_slots[slot, q])
        response = _dot(tap_matrix, jnp.concatenate([high, low, high], 0))
        responses.append((response[:BINS][None], response[BINS:][None]))
    table_even = table[:, : CHANNELS]
    table_odd = table[:, CHANNELS :]
    half = CHANNELS // 2
    turned_even = table_even * signs[0:1, : CHANNELS]
    turned_odd = jnp.concatenate([table_odd[:, half:], table_odd[:, :half]], 1) * signs[0:1, CHANNELS :]
    matrix = forward[...]
    rows = HALF * FRAMES_HERE
    weights_even = jnp.concatenate([table_even, turned_even], 0)
    weights_odd = jnp.concatenate([table_odd, turned_odd], 0)

    def product(q, h):
        real, imag = responses[q]
        z = _dot(matrix, x_slots[slot, q, h * rows : (h + 1) * rows, :]).reshape(HALF, 2, BINS, CHUNK)
        zr, zi = z[:, 0], z[:, 1]
        return zr * real - zi * imag, zr * imag + zi * real

    def joined(r, i):
        return jnp.stack([r, i], 1).reshape(2 * HALF * BINS, CHUNK).astype(BF16)

    for h in range(2):
        evens, odds = [], []
        for q in range(2):
            (ra, ia), (rb, ib) = product(q, h), product(q + 2, h)
            evens.append(joined(ra + rb, ia + ib))
            odds.append(joined(ra - rb, ia - ib))
        acc[h, :, : CHANNELS] += _dot(jnp.concatenate(evens, 1), weights_even)
        acc[h, :, CHANNELS :] += _dot(jnp.concatenate(odds, 1), weights_odd)

    def transform_back():
        for s in range(HALF // 2):
            results = []
            for ri in range(2):
                left = ri * half
                blocks = []
                for p in range(GROUPS):
                    start = (p % 2 * 4 + s) * 2 * BINS
                    block = acc[p // 2, start : start + 2 * BINS, :]
                    blocks.append(
                        jnp.concatenate(
                            [block[:, left : left + half], block[:, CHANNELS + left : CHANNELS + left + half]], 1
                        )
                    )
                high, low = _split(jnp.concatenate(blocks, 0))
                results.append(_dot(inverse[...], jnp.concatenate([high, low, high], 0)))
            for odd in range(2):
                columns = slice(odd * half, (odd + 1) * half)

                def turned(kind):
                    lines = slice(kind * 64, (kind + 1) * 64)
                    return jnp.concatenate([results[0][lines, columns], results[1][lines, columns]], 0).T

                own[pl.ds(odd * 8 + s, half, stride=16), :] = turned(0)
                own[pl.ds(odd * 8 + 4 + s, half, stride=16), :] = turned(1)
                halo[pl.ds(odd * 4 + s, half, stride=8), :] = turned(2)

    def halo_copy(target):
        return pltpu.make_async_remote_copy(
            src_ref=leaving, dst_ref=arrived, send_sem=halo_send, recv_sem=halo_recv,
            device_id=st * TA + target, device_id_type=LOGICAL,
        )

    def part_copies(message, first):
        rows = pl.ds(first, 4)

        def send(peer):
            pltpu.make_async_remote_copy(
                src_ref=message.at[peer, rows], dst_ref=out.at[me, rows], send_sem=send_sem, recv_sem=recv_sem,
                device_id=peer, device_id_type=LOGICAL,
            ).start()

        keep = pltpu.make_async_copy(message.at[me, rows], out.at[me, rows], local_sem.at[first // 4])
        keep.start()
        over_others(send)
        return keep

    @pl.when(step == STEPS - 1)
    def _():
        inverse_copy.wait()
        transform_back()
        leaving[...] = halo[...].astype(BF16)
        early[...] = own[...].reshape(CHANNELS, HALF, 128).astype(BF16)
        pl.semaphore_wait(barrier, CHANNELS - 1)

        @pl.when(ta > 0)
        def _():
            halo_copy(ta - 1).start()

        keep_early = part_copies(early, 0)

        @pl.when(ta < TA - 1)
        def _():
            halo_copy(ta).wait_recv()
            wide[...] = arrived[...].astype(F32)
            for s in range(4):
                rows = pl.ds(4 + s, CHANNELS, stride=HALF)
                own[rows, :] += wide[pl.ds(s, CHANNELS, stride=4), :]

        late[...] = own[...].reshape(CHANNELS, HALF, 128).astype(BF16)
        keep_late = part_copies(late, 4)
        keep_early.wait()
        keep_late.wait()

        @pl.when(ta > 0)
        def _():
            halo_copy(ta - 1).wait_send()

        everything = pl.ds(0, CHANNELS - 1)
        pltpu.make_async_remote_copy(
            src_ref=late.at[everything], dst_ref=out.at[everything], send_sem=send_sem, recv_sem=recv_sem,
            device_id=me, device_id_type=LOGICAL,
        ).wait()


def gather_spectra(samples, coefficients):
    x = samples.reshape(INPUTS_HERE * FRAMES_HERE, NFFT)
    whole = lambda *shape: pl.BlockSpec(shape, lambda j: (0,) * len(shape))
    left = pl.BlockSpec(memory_space=pl.ANY)
    table, signs = _channel_table(), _turn_signs()
    forward, taps, inverse = _as_bf16(_forward_matrix()), _tap_matrix(), _inverse_matrix()
    rows = CHANNELS * HALF
    return pl.pallas_call(
        spectra_kernel,
        out_shape=jax.ShapeDtypeStruct((CHANNELS, HALF, 128), BF16),
        grid=(STEPS,),
        in_specs=[left, left, left, left, whole(*signs.shape), whole(*forward.shape), whole(*taps.shape)],
        out_specs=pl.BlockSpec(memory_space=pl.ANY),
        scratch_shapes=[
            pltpu.VMEM((2, 4, INPUTS_HERE * FRAMES_HERE, CHUNK), BF16),
            pltpu.VMEM((2, 4, TAPS, CHUNK), F32),
            pltpu.VMEM((2, CHUNK, 2 * CHANNELS), BF16),
            pltpu.VMEM(inverse.shape, BF16),
            pltpu.SemaphoreType.DMA((2, 9)),
            pltpu.SemaphoreType.DMA,
            pltpu.VMEM((2, 2 * HALF * BINS, 2 * CHANNELS), F32),
            pltpu.VMEM((rows, 128), F32),
            pltpu.VMEM((rows // 2, 128), F32),
            pltpu.VMEM((CHANNELS, HALF, 128), BF16),
            pltpu.VMEM((CHANNELS, HALF, 128), BF16),
            pltpu.VMEM((rows // 2, 128), BF16),
            pltpu.VMEM((rows // 2, 128), BF16),
            pltpu.VMEM((rows // 2, 128), F32),
            pltpu.SemaphoreType.DMA((2,)),
        ]
        + [pltpu.SemaphoreType.DMA] * 4,
        compiler_params=pltpu.CompilerParams(collective_id=0, has_side_effects=True),
        name="spectra",
    )(x, coefficients, table, inverse, signs, forward, taps)


ROWS = 256


def correlate_kernel(arrived, out, spectra, packed):
    stations = spectra.shape[1]
    step = pl.program_id(0)
    block = ROWS // INPUTS_HERE

    @pl.when(step == 0)
    def _():
        group = lax.broadcasted_iota(jnp.int32, (block, 8, 128), 2) // HALF_FRAMES

        def place(b, carry):
            start = pl.multiple_of(b * block, block)
            lines = arrived[pl.ds(start * TA, block * TA)].astype(F32).reshape(block, TA, 8, 128)
            tiles = [lines[:, t] for t in range(TA)]
            for bit in (1, 2):
                shift = bit * HALF_FRAMES
                low = group // bit % 2 == 0
                for t in range(TA):
                    if t & bit == 0:
                        first, second = tiles[t], tiles[t + bit]
                        tiles[t] = jnp.where(low, first, pltpu.roll(second, shift, 2))
                        tiles[t + bit] = jnp.where(low, pltpu.roll(first, 128 - shift, 2), second)
            for p in range(GROUPS):
                for late in range(2):
                    spectra[late, pl.ds(start, block), p * 4 : (p + 1) * 4, :] = tiles[p][:, late * 4 : late * 4 + 4]
            for late in range(2):
                rows = pl.ds(pl.multiple_of(b * ROWS, ROWS), ROWS)
                values = spectra[late, pl.ds(start, block)].reshape(ROWS, 128)
                packed[rows, late * 128 : (late + 1) * 128] = values.astype(BF16)
            return carry

        lax.fori_loop(0, stations // block, place, 0)

    here = pl.ds(pl.multiple_of(step * block, block), block)
    sign = jnp.where(lax.broadcasted_iota(jnp.int32, (1, 128), 1) < 64, 1.0, -1.0)
    direct, swapped = [], []
    for late in range(2):
        values = spectra[late, here].reshape(ROWS, 128)
        direct.append(values.astype(BF16))
        swapped.append((pltpu.roll(values, 64, 1) * sign).astype(BF16))
    lines = jnp.concatenate([jnp.concatenate(direct, 1), jnp.concatenate(swapped, 1)], 0)
    result = lax.dot_general(lines, packed[...], (((1,), (1,)), ((), ())), preferred_element_type=F32)
    scaled = (result * (1.0 / 128)).astype(BF16)
    out[0, 0] = scaled[:ROWS]
    out[0, 1] = scaled[ROWS:]


def correlate(arrived):
    inputs = arrived.shape[0] // TA * INPUTS_HERE
    return pl.pallas_call(
        correlate_kernel,
        out_shape=jax.ShapeDtypeStruct((1, 2, inputs, inputs), BF16),
        grid=(inputs // ROWS,),
        in_specs=[pl.BlockSpec(arrived.shape, lambda i: (0, 0, 0))],
        out_specs=pl.BlockSpec((1, 2, ROWS, inputs), lambda i: (0, 0, i, 0)),
        scratch_shapes=[
            pltpu.VMEM((2, inputs // INPUTS_HERE, INPUTS_HERE, 128), F32),
            pltpu.VMEM((inputs, 256), BF16),
        ],
        name="correlate",
    )(arrived)


def on_device(samples, coefficients):
    return correlate(gather_spectra(samples, coefficients))


def solution(mesh):
    return jax.shard_map(
        on_device,
        mesh=mesh,
        in_specs=(P("st", "ta", None), P()),
        out_specs=P(("st", "ta"), None, None, None),
        check_vma=False,
    )
```

```python
import functools
import math

import jax
import jax.numpy as jnp
import numpy as np
from jax import lax
from jax.experimental import pallas as pl
from jax.experimental.pallas import tpu as pltpu
from jax.sharding import PartitionSpec as P

CH0 = 1024
LOGICAL = pl.DeviceIdType.LOGICAL
BF16 = jnp.bfloat16
F32 = jnp.float32

NFFT = 8192
TAPS = 16
INPUTS_HERE = 16
FRAMES_HERE = 32
CHANNELS = 256
TA = 4
BINS = 24
HALF = 8
GROUPS = 4
HALF_FRAMES = FRAMES_HERE // 2
QUARTER = NFFT // 4
CHUNK = 512
STEPS = QUARTER // CHUNK


def _as_bf16(values):
    return np.asarray(values, np.float32).astype(BF16)


def _high_low(values):
    high = _as_bf16(values)
    return high, _as_bf16(values - high.astype(np.float64))


def _bin_angles():
    return 2.0 * np.pi * (np.arange(BINS) + 0.5) / (2 * BINS)


def _forward_matrix():
    angles = _bin_angles()[:, None] * np.arange(FRAMES_HERE)[None, :]
    parts = np.stack([np.cos(angles), -np.sin(angles)])
    block = np.zeros((HALF, 2, BINS, HALF, FRAMES_HERE))
    for i in range(HALF):
        block[i, :, :, i, :] = parts
    return block.reshape(2 * HALF * BINS, HALF * FRAMES_HERE)


def _tap_matrix():
    angles = _bin_angles()[:, None] * np.arange(TAPS)[None, :]
    taps = np.concatenate([np.cos(angles), np.sin(angles)])
    high, low = _high_low(taps)
    return np.concatenate([high, high, low], 1)


def _inverse_matrix():
    scale = (2.0 / (2 * BINS)) * NFFT ** -0.5
    rows = np.zeros((3, GROUPS, HALF_FRAMES, GROUPS, 2, BINS))
    for kind, first in enumerate((0, HALF_FRAMES, -HALF_FRAMES)):
        frames = first + np.arange(HALF_FRAMES)
        angles = _bin_angles()[:, None] * frames[None, :]
        values = scale * np.stack([np.cos(angles), -np.sin(angles)])
        if first < 0:
            values[:, :, frames <= -TAPS] = 0.0
        for p in range(GROUPS):
            rows[kind, p, :, p] = np.moveaxis(values, 2, 0)
    high, low = _high_low(rows.reshape(3 * GROUPS * HALF_FRAMES, 2 * GROUPS * BINS))
    return np.concatenate([high, high, low], 1)


def _channel_table():
    positions = np.arange(QUARTER)[:, None]
    columns = []
    for odd in range(2):
        channels = CH0 + np.arange(odd, CHANNELS, 2)[None, :]
        angles = 2.0 * np.pi * (positions * channels % NFFT) / NFFT
        columns += [np.cos(angles), -np.sin(angles)]
    return _as_bf16(np.concatenate(columns, 1))


def _turn_signs():
    even = np.where(np.arange(0, CHANNELS, 2) % 4 == 0, 1.0, -1.0)
    odd = np.where(np.arange(1, CHANNELS, 2) % 4 == 1, 1.0, -1.0)
    rows = np.concatenate([even, even, odd, -odd])[None, :]
    return _as_bf16(np.broadcast_to(rows, (16, 2 * CHANNELS)))


def _dot(a, b):
    return jnp.dot(a, b, preferred_element_type=F32)


def _split(values):
    high = values.astype(BF16)
    return high, (values - high.astype(F32)).astype(BF16)


def spectra_kernel(
    x, coefficients, table_all, inverse_all, signs, forward, taps,
    out,
    x_slots, c_slots, table_slots, inverse, in_sems, inverse_sem, kept, kept_table, acc, own, halo, early, late, leaving, arrived, wide, local_sem, halo_send, halo_recv, send_sem, recv_sem,
):
    step = pl.program_id(0)
    st = lax.axis_index("st")
    ta = lax.axis_index("ta")
    me = st * TA + ta
    barrier = pltpu.get_barrier_semaphore()

    def greet(peer, carry):
        pl.semaphore_signal(barrier, inc=1, device_id=peer, device_id_type=LOGICAL)
        return carry

    def inputs(j):
        slot = lax.rem(j, 2)
        copies = []
        for q in range(4):
            columns = pl.ds(pl.multiple_of((q * STEPS + j) * CHUNK, CHUNK), CHUNK)
            copies.append(pltpu.make_async_copy(x.at[:, columns], x_slots.at[slot, q], in_sems.at[slot, q]))
            copies.append(
                pltpu.make_async_copy(coefficients.at[:, columns], c_slots.at[slot, q], in_sems.at[slot, 4 + q])
            )
        lines = pl.ds(pl.multiple_of(j * CHUNK, CHUNK), CHUNK)
        copies.append(pltpu.make_async_copy(table_all.at[lines], table_slots.at[slot], in_sems.at[slot, 8]))
        return copies

    inverse_copy = pltpu.make_async_copy(inverse_all, inverse, inverse_sem)

    @pl.when(step == 0)
    def _():
        for copy in inputs(step):
            copy.start()
        inverse_copy.start()
        lax.fori_loop(me + 1, CHANNELS, greet, 0)
        lax.fori_loop(0, me, greet, 0)
        acc[...] = jnp.zeros_like(acc)

    @pl.when(step < STEPS - 1)
    def _():
        for copy in inputs(step + 1):
            copy.start()

    for copy in inputs(step):
        copy.wait()
    slot = lax.rem(step, 2)
    table = table_slots[slot]
    tap_matrix = taps[...]
    responses = []
    for q in range(4):
        high, low = _split(c_slots[slot, q])
        response = _dot(tap_matrix, jnp.concatenate([high, low, high], 0))
        responses.append((response[:BINS][None], response[BINS:][None]))
    table_even = table[:, : CHANNELS]
    table_odd = table[:, CHANNELS :]
    half = CHANNELS // 2
    turned_even = table_even * signs[0:1, : CHANNELS]
    turned_odd = jnp.concatenate([table_odd[:, half:], table_odd[:, :half]], 1) * signs[0:1, CHANNELS :]
    matrix = forward[...]
    rows = HALF * FRAMES_HERE
    weights_even = jnp.concatenate([table_even, turned_even], 0)
    weights_odd = jnp.concatenate([table_odd, turned_odd], 0)

    def product(q, h):
        real, imag = responses[q]
        z = _dot(matrix, x_slots[slot, q, h * rows : (h + 1) * rows, :]).reshape(HALF, 2, BINS, CHUNK)
        zr, zi = z[:, 0], z[:, 1]
        return zr * real - zi * imag, zr * imag + zi * real

    def joined(r, i):
        return jnp.stack([r, i], 1).reshape(2 * HALF * BINS, CHUNK).astype(BF16)

    for h in range(2):
        evens, odds = [], []
        for q in range(2):
            (ra, ia), (rb, ib) = product(q, h), product(q + 2, h)
            evens.append(joined(ra + rb, ia + ib))
            odds.append(joined(ra - rb, ia - ib))
        acc[h] += _dot(jnp.concatenate(evens, 1), weights_even)
        kept[h, :, pl.ds(pl.multiple_of(step * 2 * CHUNK, 2 * CHUNK), 2 * CHUNK)] = jnp.concatenate(odds, 1)

    kept_table[pl.ds(pl.multiple_of(step * 2 * CHUNK, 2 * CHUNK), 2 * CHUNK), :] = weights_odd

    def transform_back(parity):
        for pair in range(2):
            results = []
            for ri in range(2):
                sides = []
                for s in (2 * pair, 2 * pair + 1):
                    blocks = []
                    for p in range(GROUPS):
                        start = (p % 2 * 4 + s) * 2 * BINS
                        blocks.append(acc[p // 2, start : start + 2 * BINS, ri * half : (ri + 1) * half])
                    sides.append(jnp.concatenate(blocks, 0))
                high, low = _split(jnp.concatenate(sides, 1))
                results.append(_dot(inverse[...], jnp.concatenate([high, low, high], 0)))
            for side in range(2):
                s = 2 * pair + side
                columns = slice(side * half, (side + 1) * half)

                def turned(kind):
                    lines = slice(kind * 64, (kind + 1) * 64)
                    return jnp.concatenate([results[0][lines, columns], results[1][lines, columns]], 0).T

                own[parity, pl.ds(s, half, stride=8), :] = turned(0)
                own[parity, pl.ds(4 + s, half, stride=8), :] = turned(1)
                halo[pl.ds(s, half, stride=4), :] = turned(2)
        leaving[parity] = halo[...].astype(BF16)

    def halo_copy(parity, target):
        return pltpu.make_async_remote_copy(
            src_ref=leaving.at[parity], dst_ref=arrived.at[parity], send_sem=halo_send.at[parity],
            recv_sem=halo_recv.at[parity], device_id=st * TA + target, device_id_type=LOGICAL,
        )

    place = me // 2
    other = [lax.rem(me, 2), 1 - lax.rem(me, 2)]

    def keep_copy(message, parity, first):
        rows = pl.ds(first, 4)
        return pltpu.make_async_copy(message.at[parity, place, rows], out.at[me, rows], local_sem.at[first // 4])

    def send_part(message, parity, first):
        rows = pl.ds(first, 4)

        def send(r, carry):
            pltpu.make_async_remote_copy(
                src_ref=message.at[parity, r, rows], dst_ref=out.at[me, rows], send_sem=send_sem, recv_sem=recv_sem,
                device_id=2 * r + parity, device_id_type=LOGICAL,
            ).start()
            return carry

        @pl.when(other[parity] == 0)
        def _():
            keep_copy(message, parity, first).start()

        lax.fori_loop(place + 1, half, send, 0)
        lax.fori_loop(0, place + other[parity], send, 0)

    def message_values(parity):
        return own[parity].reshape(half, HALF, 128).astype(BF16)

    def start_halo(parity):
        @pl.when(ta > 0)
        def _():
            halo_copy(parity, ta - 1).start()

    def add_halo(parity):
        @pl.when(ta < TA - 1)
        def _():
            halo_copy(parity, ta).wait_recv()
            wide[...] = arrived[parity].astype(F32)
            for s in range(4):
                rows = pl.ds(4 + s, half, stride=HALF)
                own[parity, rows, :] += wide[pl.ds(s, half, stride=4), :]

    @pl.when(step == STEPS - 1)
    def _():
        inverse_copy.wait()
        transform_back(0)
        pl.semaphore_wait(barrier, CHANNELS - 1)
        start_halo(0)
        early[0] = message_values(0)
        send_part(early, 0, 0)
        for h in range(2):
            acc[h] = _dot(kept[h], kept_table[...])
        add_halo(0)
        late[0] = message_values(0)
        send_part(late, 0, 4)
        transform_back(1)
        start_halo(1)
        early[1] = message_values(1)
        send_part(early, 1, 0)
        add_halo(1)
        late[1] = message_values(1)
        send_part(late, 1, 4)
        for parity in range(2):

            @pl.when(other[parity] == 0)
            def _():
                keep_copy(early, parity, 0).wait()
                keep_copy(late, parity, 4).wait()

        @pl.when(ta > 0)
        def _():
            halo_copy(0, ta - 1).wait_send()
            halo_copy(1, ta - 1).wait_send()

        everything = pl.ds(0, CHANNELS - 1)
        pltpu.make_async_remote_copy(
            src_ref=out.at[everything], dst_ref=out.at[everything], send_sem=send_sem, recv_sem=recv_sem,
            device_id=me, device_id_type=LOGICAL,
        ).wait()


def gather_spectra(samples, coefficients):
    x = samples.reshape(INPUTS_HERE * FRAMES_HERE, NFFT)
    whole = lambda *shape: pl.BlockSpec(shape, lambda j: (0,) * len(shape))
    left = pl.BlockSpec(memory_space=pl.ANY)
    table, signs = _channel_table(), _turn_signs()
    forward, taps, inverse = _as_bf16(_forward_matrix()), _tap_matrix(), _inverse_matrix()
    rows = CHANNELS * HALF
    return pl.pallas_call(
        spectra_kernel,
        out_shape=jax.ShapeDtypeStruct((CHANNELS, HALF, 128), BF16),
        grid=(STEPS,),
        in_specs=[left, left, left, left, whole(*signs.shape), whole(*forward.shape), whole(*taps.shape)],
        out_specs=pl.BlockSpec(memory_space=pl.ANY),
        scratch_shapes=[
            pltpu.VMEM((2, 4, INPUTS_HERE * FRAMES_HERE, CHUNK), BF16),
            pltpu.VMEM((2, 4, TAPS, CHUNK), F32),
            pltpu.VMEM((2, CHUNK, 2 * CHANNELS), BF16),
            pltpu.VMEM(inverse.shape, BF16),
            pltpu.SemaphoreType.DMA((2, 9)),
            pltpu.SemaphoreType.DMA,
            pltpu.VMEM((2, 2 * HALF * BINS, NFFT // 2), BF16),
            pltpu.VMEM((NFFT // 2, CHANNELS), BF16),
            pltpu.VMEM((2, 2 * HALF * BINS, CHANNELS), F32),
            pltpu.VMEM((2, rows // 2, 128), F32),
            pltpu.VMEM((rows // 4, 128), F32),
            pltpu.VMEM((2, CHANNELS // 2, HALF, 128), BF16),
            pltpu.VMEM((2, CHANNELS // 2, HALF, 128), BF16),
            pltpu.VMEM((2, rows // 4, 128), BF16),
            pltpu.VMEM((2, rows // 4, 128), BF16),
            pltpu.VMEM((rows // 4, 128), F32),
        ]
        + [pltpu.SemaphoreType.DMA((2,))] * 3
        + [pltpu.SemaphoreType.DMA] * 2,
        compiler_params=pltpu.CompilerParams(collective_id=0, has_side_effects=True),
        name="spectra",
    )(x, coefficients, table, inverse, signs, forward, taps)


ROWS = 256


def correlate_kernel(arrived, out, spectra, packed):
    stations = spectra.shape[1]
    step = pl.program_id(0)
    block = ROWS // INPUTS_HERE

    @pl.when(step == 0)
    def _():
        group = lax.broadcasted_iota(jnp.int32, (block, 8, 128), 2) // HALF_FRAMES

        def place(b, carry):
            start = pl.multiple_of(b * block, block)
            lines = arrived[pl.ds(start * TA, block * TA)].astype(F32).reshape(block, TA, 8, 128)
            tiles = [lines[:, t] for t in range(TA)]
            for bit in (1, 2):
                shift = bit * HALF_FRAMES
                low = group // bit % 2 == 0
                for t in range(TA):
                    if t & bit == 0:
                        first, second = tiles[t], tiles[t + bit]
                        tiles[t] = jnp.where(low, first, pltpu.roll(second, shift, 2))
                        tiles[t + bit] = jnp.where(low, pltpu.roll(first, 128 - shift, 2), second)
            for p in range(GROUPS):
                for late in range(2):
                    spectra[late, pl.ds(start, block), p * 4 : (p + 1) * 4, :] = tiles[p][:, late * 4 : late * 4 + 4]
            for late in range(2):
                rows = pl.ds(pl.multiple_of(b * ROWS, ROWS), ROWS)
                values = spectra[late, pl.ds(start, block)].reshape(ROWS, 128)
                packed[rows, late * 128 : (late + 1) * 128] = values.astype(BF16)
            return carry

        lax.fori_loop(0, stations // block, place, 0, unroll=4)

    here = pl.ds(pl.multiple_of(step * block, block), block)
    sign = jnp.where(lax.broadcasted_iota(jnp.int32, (1, 128), 1) < 64, 1.0, -1.0)
    direct, swapped = [], []
    for late in range(2):
        values = spectra[late, here].reshape(ROWS, 128)
        direct.append(values.astype(BF16))
        swapped.append((pltpu.roll(values, 64, 1) * sign).astype(BF16))
    lines = jnp.concatenate([jnp.concatenate(direct, 1), jnp.concatenate(swapped, 1)], 0)
    result = lax.dot_general(lines, packed[...], (((1,), (1,)), ((), ())), preferred_element_type=F32)
    scaled = (result * (1.0 / 128)).astype(BF16)
    out[0, 0] = scaled[:ROWS]
    out[0, 1] = scaled[ROWS:]


def correlate(arrived):
    inputs = arrived.shape[0] // TA * INPUTS_HERE
    return pl.pallas_call(
        correlate_kernel,
        out_shape=jax.ShapeDtypeStruct((1, 2, inputs, inputs), BF16),
        grid=(inputs // ROWS,),
        in_specs=[pl.BlockSpec(arrived.shape, lambda i: (0, 0, 0))],
        out_specs=pl.BlockSpec((1, 2, ROWS, inputs), lambda i: (0, 0, i, 0)),
        scratch_shapes=[
            pltpu.VMEM((2, inputs // INPUTS_HERE, INPUTS_HERE, 128), F32),
            pltpu.VMEM((inputs, 256), BF16),
        ],
        name="correlate",
    )(arrived)


def on_device(samples, coefficients):
    return correlate(gather_spectra(samples, coefficients))


def solution(mesh):
    return jax.shard_map(
        on_device,
        mesh=mesh,
        in_specs=(P("st", "ta", None), P()),
        out_specs=P(("st", "ta"), None, None, None),
        check_vma=False,
    )
```

```python
import functools
import math

import jax
import jax.numpy as jnp
import numpy as np
from jax import lax
from jax.experimental import pallas as pl
from jax.experimental.pallas import tpu as pltpu
from jax.sharding import PartitionSpec as P

CH0 = 1024
LOGICAL = pl.DeviceIdType.LOGICAL
BF16 = jnp.bfloat16
F32 = jnp.float32

NFFT = 8192
TAPS = 16
INPUTS_HERE = 16
FRAMES_HERE = 32
CHANNELS = 256
TA = 4
BINS = 24
HALF = 8
GROUPS = 4
HALF_FRAMES = FRAMES_HERE // 2
QUARTER = NFFT // 4
CHUNK = 512
STEPS = QUARTER // CHUNK


def _as_bf16(values):
    return np.asarray(values, np.float32).astype(BF16)


def _high_low(values):
    high = _as_bf16(values)
    return high, _as_bf16(values - high.astype(np.float64))


def _bin_angles():
    return 2.0 * np.pi * (np.arange(BINS) + 0.5) / (2 * BINS)


def _forward_matrix():
    angles = _bin_angles()[:, None] * np.arange(FRAMES_HERE)[None, :]
    parts = np.stack([np.cos(angles), -np.sin(angles)])
    block = np.zeros((HALF, 2, BINS, HALF, FRAMES_HERE))
    for i in range(HALF):
        block[i, :, :, i, :] = parts
    return block.reshape(2 * HALF * BINS, HALF * FRAMES_HERE)


def _tap_matrix():
    angles = _bin_angles()[:, None] * np.arange(TAPS)[None, :]
    taps = np.concatenate([np.cos(angles), np.sin(angles)])
    high, low = _high_low(taps)
    return np.concatenate([high, high, low], 1)


def _inverse_matrix():
    scale = (2.0 / (2 * BINS)) * NFFT ** -0.5
    rows = np.zeros((3, GROUPS, HALF_FRAMES, GROUPS, 2, BINS))
    for kind, first in enumerate((0, HALF_FRAMES, -HALF_FRAMES)):
        frames = first + np.arange(HALF_FRAMES)
        angles = _bin_angles()[:, None] * frames[None, :]
        values = scale * np.stack([np.cos(angles), -np.sin(angles)])
        if first < 0:
            values[:, :, frames <= -TAPS] = 0.0
        for p in range(GROUPS):
            rows[kind, p, :, p] = np.moveaxis(values, 2, 0)
    high, low = _high_low(rows.reshape(3 * GROUPS * HALF_FRAMES, 2 * GROUPS * BINS))
    return np.concatenate([high, high, low], 1)


def _channel_table():
    positions = np.arange(QUARTER)[:, None]
    columns = []
    for odd in range(2):
        channels = CH0 + np.arange(odd, CHANNELS, 2)[None, :]
        angles = 2.0 * np.pi * (positions * channels % NFFT) / NFFT
        columns += [np.cos(angles), -np.sin(angles)]
    return _as_bf16(np.concatenate(columns, 1))


def _turn_signs():
    even = np.where(np.arange(0, CHANNELS, 2) % 4 == 0, 1.0, -1.0)
    odd = np.where(np.arange(1, CHANNELS, 2) % 4 == 1, 1.0, -1.0)
    rows = np.concatenate([even, even, odd, -odd])[None, :]
    return _as_bf16(np.broadcast_to(rows, (16, 2 * CHANNELS)))


def _dot(a, b):
    return jnp.dot(a, b, preferred_element_type=F32)


def _split(values):
    high = values.astype(BF16)
    return high, (values - high.astype(F32)).astype(BF16)


def spectra_kernel(
    x, coefficients, table_all, inverse_all, signs, forward, taps,
    out,
    x_slots, c_slots, table_slots, inverse, in_sems, inverse_sem, kept, kept_table, acc, own, halo, early, late, leaving, arrived, wide, local_sem, halo_send, halo_recv, send_sem, recv_sem,
):
    step = pl.program_id(0)
    st = lax.axis_index("st")
    ta = lax.axis_index("ta")
    me = st * TA + ta
    barrier = pltpu.get_barrier_semaphore()

    def greet(peer, carry):
        pl.semaphore_signal(barrier, inc=1, device_id=peer, device_id_type=LOGICAL)
        return carry

    def inputs(j):
        slot = lax.rem(j, 2)
        copies = []
        for q in range(4):
            columns = pl.ds(pl.multiple_of((q * STEPS + j) * CHUNK, CHUNK), CHUNK)
            copies.append(pltpu.make_async_copy(x.at[:, columns], x_slots.at[slot, q], in_sems.at[slot, q]))
            copies.append(
                pltpu.make_async_copy(coefficients.at[:, columns], c_slots.at[slot, q], in_sems.at[slot, 4 + q])
            )
        lines = pl.ds(pl.multiple_of(j * CHUNK, CHUNK), CHUNK)
        copies.append(pltpu.make_async_copy(table_all.at[lines], table_slots.at[slot], in_sems.at[slot, 8]))
        return copies

    inverse_copy = pltpu.make_async_copy(inverse_all, inverse, inverse_sem)

    @pl.when(step == 0)
    def _():
        for copy in inputs(step):
            copy.start()
        inverse_copy.start()
        lax.fori_loop(me + 1, CHANNELS, greet, 0)
        lax.fori_loop(0, me, greet, 0)
        acc[...] = jnp.zeros_like(acc)

    @pl.when(step < STEPS - 1)
    def _():
        for copy in inputs(step + 1):
            copy.start()

    for copy in inputs(step):
        copy.wait()
    slot = lax.rem(step, 2)
    table = table_slots[slot]
    tap_matrix = taps[...]
    responses = []
    for q in range(4):
        high, low = _split(c_slots[slot, q])
        response = _dot(tap_matrix, jnp.concatenate([high, low, high], 0))
        responses.append((response[:BINS][None], response[BINS:][None]))
    table_even = table[:, : CHANNELS]
    table_odd = table[:, CHANNELS :]
    half = CHANNELS // 2
    turned_even = table_even * signs[0:1, : CHANNELS]
    turned_odd = jnp.concatenate([table_odd[:, half:], table_odd[:, :half]], 1) * signs[0:1, CHANNELS :]
    matrix = forward[...]
    rows = HALF * FRAMES_HERE
    weights_even = jnp.concatenate([table_even, turned_even], 0)
    weights_odd = jnp.concatenate([table_odd, turned_odd], 0)

    def product(q, h):
        real, imag = responses[q]
        z = _dot(matrix, x_slots[slot, q, h * rows : (h + 1) * rows, :]).reshape(HALF, 2, BINS, CHUNK)
        zr, zi = z[:, 0], z[:, 1]
        return zr * real - zi * imag, zr * imag + zi * real

    def joined(r, i):
        return jnp.stack([r, i], 1).reshape(2 * HALF * BINS, CHUNK).astype(BF16)

    for h in range(2):
        evens, odds = [], []
        for q in range(2):
            (ra, ia), (rb, ib) = product(q, h), product(q + 2, h)
            evens.append(joined(ra + rb, ia + ib))
            odds.append(joined(ra - rb, ia - ib))
        acc[h] += _dot(jnp.concatenate(evens, 1), weights_even)
        kept[h, :, pl.ds(pl.multiple_of(step * 2 * CHUNK, 2 * CHUNK), 2 * CHUNK)] = jnp.concatenate(odds, 1)

    kept_table[pl.ds(pl.multiple_of(step * 2 * CHUNK, 2 * CHUNK), 2 * CHUNK), :] = weights_odd

    def transform_back(parity):
        for pair in range(2):
            results = []
            for ri in range(2):
                sides = []
                for s in (2 * pair, 2 * pair + 1):
                    blocks = []
                    for p in range(GROUPS):
                        start = (p % 2 * 4 + s) * 2 * BINS
                        blocks.append(acc[p // 2, start : start + 2 * BINS, ri * half : (ri + 1) * half])
                    sides.append(jnp.concatenate(blocks, 0))
                high, low = _split(jnp.concatenate(sides, 1))
                results.append(_dot(inverse[...], jnp.concatenate([high, low, high], 0)))
            for side in range(2):
                s = 2 * pair + side
                columns = slice(side * half, (side + 1) * half)

                def turned(kind):
                    lines = slice(kind * 64, (kind + 1) * 64)
                    return jnp.concatenate([results[0][lines, columns], results[1][lines, columns]], 0).T

                own[parity, pl.ds(s, half, stride=8), :] = turned(0)
                own[parity, pl.ds(4 + s, half, stride=8), :] = turned(1)
                halo[pl.ds(s, half, stride=4), :] = turned(2)
        leaving[parity] = halo[...].astype(BF16)

    def halo_copy(parity, target):
        return pltpu.make_async_remote_copy(
            src_ref=leaving.at[parity], dst_ref=arrived.at[parity], send_sem=halo_send.at[parity],
            recv_sem=halo_recv.at[parity], device_id=st * TA + target, device_id_type=LOGICAL,
        )

    place = me // 2
    other = [lax.rem(me, 2), 1 - lax.rem(me, 2)]

    def keep_copy(message, parity, first):
        rows = pl.ds(first, 4)
        return pltpu.make_async_copy(message.at[parity, place, rows], out.at[me, rows], local_sem.at[first // 4])

    def send_part(message, parity, first):
        rows = pl.ds(first, 4)

        def send(r, carry):
            pltpu.make_async_remote_copy(
                src_ref=message.at[parity, r, rows], dst_ref=out.at[me, rows], send_sem=send_sem, recv_sem=recv_sem,
                device_id=2 * r + parity, device_id_type=LOGICAL,
            ).start()
            return carry

        @pl.when(other[parity] == 0)
        def _():
            keep_copy(message, parity, first).start()

        lax.fori_loop(place + 1, half, send, 0)
        lax.fori_loop(0, place + other[parity], send, 0)

    def message_values(parity):
        return own[parity].reshape(half, HALF, 128).astype(BF16)

    def start_halo(parity):
        @pl.when(ta > 0)
        def _():
            halo_copy(parity, ta - 1).start()

    def add_halo(parity):
        @pl.when(ta < TA - 1)
        def _():
            halo_copy(parity, ta).wait_recv()
            wide[...] = arrived[parity].astype(F32)
            for s in range(4):
                rows = pl.ds(4 + s, half, stride=HALF)
                own[parity, rows, :] += wide[pl.ds(s, half, stride=4), :]

    @pl.when(step == STEPS - 1)
    def _():
        inverse_copy.wait()
        transform_back(0)
        pl.semaphore_wait(barrier, CHANNELS - 1)
        start_halo(0)
        early[0] = message_values(0)
        send_part(early, 0, 0)
        for h in range(2):
            acc[h] = _dot(kept[h], kept_table[...])
        add_halo(0)
        late[0] = message_values(0)
        send_part(late, 0, 4)
        transform_back(1)
        start_halo(1)
        early[1] = message_values(1)
        send_part(early, 1, 0)
        add_halo(1)
        late[1] = message_values(1)
        send_part(late, 1, 4)
        for parity in range(2):

            @pl.when(other[parity] == 0)
            def _():
                keep_copy(early, parity, 0).wait()
                keep_copy(late, parity, 4).wait()

        @pl.when(ta > 0)
        def _():
            halo_copy(0, ta - 1).wait_send()
            halo_copy(1, ta - 1).wait_send()

        everything = pl.ds(0, CHANNELS - 1)
        pltpu.make_async_remote_copy(
            src_ref=out.at[everything], dst_ref=out.at[everything], send_sem=send_sem, recv_sem=recv_sem,
            device_id=me, device_id_type=LOGICAL,
        ).wait()


def gather_spectra(samples, coefficients):
    x = samples.reshape(INPUTS_HERE * FRAMES_HERE, NFFT)
    whole = lambda *shape: pl.BlockSpec(shape, lambda j: (0,) * len(shape))
    left = pl.BlockSpec(memory_space=pl.ANY)
    table, signs = _channel_table(), _turn_signs()
    forward, taps, inverse = _as_bf16(_forward_matrix()), _tap_matrix(), _inverse_matrix()
    rows = CHANNELS * HALF
    return pl.pallas_call(
        spectra_kernel,
        out_shape=jax.ShapeDtypeStruct((CHANNELS, HALF, 128), BF16),
        grid=(STEPS,),
        in_specs=[left, left, left, left, whole(*signs.shape), whole(*forward.shape), whole(*taps.shape)],
        out_specs=pl.BlockSpec(memory_space=pl.ANY),
        scratch_shapes=[
            pltpu.VMEM((2, 4, INPUTS_HERE * FRAMES_HERE, CHUNK), BF16),
            pltpu.VMEM((2, 4, TAPS, CHUNK), F32),
            pltpu.VMEM((2, CHUNK, 2 * CHANNELS), BF16),
            pltpu.VMEM(inverse.shape, BF16),
            pltpu.SemaphoreType.DMA((2, 9)),
            pltpu.SemaphoreType.DMA,
            pltpu.VMEM((2, 2 * HALF * BINS, NFFT // 2), BF16),
            pltpu.VMEM((NFFT // 2, CHANNELS), BF16),
            pltpu.VMEM((2, 2 * HALF * BINS, CHANNELS), F32),
            pltpu.VMEM((2, rows // 2, 128), F32),
            pltpu.VMEM((rows // 4, 128), F32),
            pltpu.VMEM((2, CHANNELS // 2, HALF, 128), BF16),
            pltpu.VMEM((2, CHANNELS // 2, HALF, 128), BF16),
            pltpu.VMEM((2, rows // 4, 128), BF16),
            pltpu.VMEM((2, rows // 4, 128), BF16),
            pltpu.VMEM((rows // 4, 128), F32),
        ]
        + [pltpu.SemaphoreType.DMA((2,))] * 3
        + [pltpu.SemaphoreType.DMA] * 2,
        compiler_params=pltpu.CompilerParams(collective_id=0, has_side_effects=True),
        name="spectra",
    )(x, coefficients, table, inverse, signs, forward, taps)


ROWS = 128


def correlate_kernel(arrived, out, spectra, packed):
    stations = spectra.shape[1]
    step = pl.program_id(0)
    block = ROWS // INPUTS_HERE

    @pl.when(step == 0)
    def _():
        group = lax.broadcasted_iota(jnp.int32, (block, 8, 128), 2) // HALF_FRAMES

        def place(b, carry):
            start = pl.multiple_of(b * block, block)
            lines = arrived[pl.ds(start * TA, block * TA)].astype(F32).reshape(block, TA, 8, 128)
            tiles = [lines[:, t] for t in range(TA)]
            for bit in (1, 2):
                shift = bit * HALF_FRAMES
                low = group // bit % 2 == 0
                for t in range(TA):
                    if t & bit == 0:
                        first, second = tiles[t], tiles[t + bit]
                        tiles[t] = jnp.where(low, first, pltpu.roll(second, shift, 2))
                        tiles[t + bit] = jnp.where(low, pltpu.roll(first, 128 - shift, 2), second)
            for p in range(GROUPS):
                for late in range(2):
                    spectra[late, pl.ds(start, block), p * 4 : (p + 1) * 4, :] = tiles[p][:, late * 4 : late * 4 + 4]
            for late in range(2):
                rows = pl.ds(pl.multiple_of(b * ROWS, ROWS), ROWS)
                values = spectra[late, pl.ds(start, block)].reshape(ROWS, 128)
                packed[rows, late * 128 : (late + 1) * 128] = values.astype(BF16)
            return carry

        lax.fori_loop(0, stations // block, place, 0, unroll=8)

    here = pl.ds(pl.multiple_of(step * block, block), block)
    sign = jnp.where(lax.broadcasted_iota(jnp.int32, (1, 128), 1) < 64, 1.0, -1.0)
    direct, swapped = [], []
    for late in range(2):
        values = spectra[late, here].reshape(ROWS, 128)
        direct.append(values.astype(BF16))
        swapped.append((pltpu.roll(values, 64, 1) * sign).astype(BF16))
    lines = jnp.concatenate([jnp.concatenate(direct, 1), jnp.concatenate(swapped, 1)], 0)
    result = lax.dot_general(lines, packed[...], (((1,), (1,)), ((), ())), preferred_element_type=F32)
    scaled = (result * (1.0 / 128)).astype(BF16)
    out[0, 0] = scaled[:ROWS]
    out[0, 1] = scaled[ROWS:]


def correlate(arrived):
    inputs = arrived.shape[0] // TA * INPUTS_HERE
    return pl.pallas_call(
        correlate_kernel,
        out_shape=jax.ShapeDtypeStruct((1, 2, inputs, inputs), BF16),
        grid=(inputs // ROWS,),
        in_specs=[pl.BlockSpec(arrived.shape, lambda i: (0, 0, 0))],
        out_specs=pl.BlockSpec((1, 2, ROWS, inputs), lambda i: (0, 0, i, 0)),
        scratch_shapes=[
            pltpu.VMEM((2, inputs // INPUTS_HERE, INPUTS_HERE, 128), F32),
            pltpu.VMEM((inputs, 256), BF16),
        ],
        name="correlate",
    )(arrived)


def on_device(samples, coefficients):
    return correlate(gather_spectra(samples, coefficients))


def solution(mesh):
    return jax.shard_map(
        on_device,
        mesh=mesh,
        in_specs=(P("st", "ta", None), P()),
        out_specs=P(("st", "ta"), None, None, None),
        check_vma=False,
    )
```
